512 devices in a mesh: leaf: 32 (over z_hi, y, core), mat: 16 (over x, z_lo).
Axes of the slice: x: 4, y: 4, z: 16 (z_hi: 4, z_lo: 4; z = z_hi * 4 + z_lo), core: 2. Of those that a mesh axis runs over, the one named last changes fastest.
Arguments:
- leaf_value: float32 [256, 1024, 1024], P('leaf', 'mat'), as said below
- section_cost: float32 [1024, 1024], P('mat'), as said below
- input_cost: float32 [256, 256], replicated, as said below
- dynamics: float32 [1024, 1024], P('mat'), may hold values from -0.1875 to 0.1875
- input_map: float32 [1024, 256], replicated, may hold values from -0.1875 to 0.1875
- parent_of: int32 [256], replicated, may hold values from 0 to 63, as said below
- prob_weight: int32 [256], replicated, may hold values from 1 to 16
- parent_state: float32 [64, 1024], P('leaf', 'mat'), may hold values from -6 to 6
- disturbance: float32 [256, 1024], P('leaf', 'mat'), may hold values from -6 to 6
Outputs:
- parent_value: float32 [64, 1024, 1024], P('leaf', 'mat')
- parent_gain: float32 [64, 1024, 256], P('leaf', 'mat')
- child_state: float32 [256, 1024], P('leaf', 'mat')
The draws below stay inside these ranges and needn't reach their ends.
Inputs may be any that keep to these rules, and one draw needn't show every extreme that they name: Each leaf_value[l] is symmetric positive definite. `section_cost`: symmetric positive definite. `input_cost`: symmetric positive definite. `parent_of`: every parent has exactly 4 children; the parent of a leaf among the 8 leaves of one leaf index is one of that index's 2 parents, the last parent of the index before, or the first parent of the index after; each leaf index except the ends holds a child of both neighbours' parents.
All inputs are finite; a program needn't handle non-finite values.
Results may differ from the reference program's by a relative error of at most 0.000075.
Values sent between devices are 32-bit elements; how exact they have to be, the bound alone decides.
No kernel may reach another device: no remote copies, remote signals or barrier semaphores. Data moves between devices by JAX's collectives and lax.ppermute only.
A program may use at most 64 MiB of HBM per device.

```python
import jax
import jax.numpy as jnp
from jax import lax

N = 1024
M = 256
LEAF_DEV = 8
LEAVES = 256
PARENTS = 64


def spd_matrix(key, order, spread, low, high):
    first, second = jax.random.split(key)
    noise = jax.random.normal(first, (order, order), jnp.float32) * (spread / order ** 0.5)
    sym = (noise + noise.T) * 0.7071
    diag = jax.random.uniform(second, (order,), jnp.float32, low, high)
    return sym + jnp.diag(diag)


def draw_leaf_value(key, part):
    base = jax.random.fold_in(key, 101)
    keys = jax.random.split(base, LEAVES)
    return jax.vmap(lambda k: spd_matrix(k, N, 0.7, 2.0, 4.0))(keys)


def draw_section_cost(key, part):
    base = jax.random.fold_in(key, 202)
    return spd_matrix(base, N, 0.3, 1.0, 2.0)


def draw_input_cost(key, part):
    base = jax.random.fold_in(key, 303)
    return spd_matrix(base, M, 0.3, 1.0, 3.0)


def draw_parent_of(key, part):
    base = jax.random.fold_in(key, 404)
    first, second = jax.random.split(base)
    groups = LEAVES // LEAF_DEV
    labels = jnp.arange(LEAVES, dtype=jnp.int32) // 4
    bounds = jnp.arange(groups - 1, dtype=jnp.int32)
    upper = jax.random.randint(first, (groups - 1,), 2, 4, dtype=jnp.int32) + (LEAF_DEV - 4)
    lower = jax.random.randint(second, (groups - 1,), 0, 2, dtype=jnp.int32)
    source = bounds * LEAF_DEV + upper
    target = (bounds + 1) * LEAF_DEV + lower
    return labels.at[source].set(labels[target]).at[target].set(labels[source])


def with_ends(result, rng, low, largest):
    shape = result.shape
    index_at = [jax.random.randint(jax.random.fold_in(rng, axis), (), 0, shape[axis]) for axis in range(len(shape))]
    result = result.at[tuple(index_at)].set(low)
    longest = shape.index(max(shape))
    index_at[longest] = (index_at[longest] + 1) % shape[longest]
    return result.at[tuple(index_at)].set(largest)


def steps_of(rng, dims, cuts, low, largest):
    loudness = 1.0
    for position, shards_of in cuts:
        draws = jax.random.uniform(jax.random.fold_in(jax.random.fold_in(rng, 6), position), (shards_of,), jnp.float32, low / len(cuts), largest / len(cuts))
        loudness = loudness * jnp.repeat(jnp.exp(draws), dims[position] // shards_of).reshape((-1,) + (1,) * (len(dims) - 1 - position))
    return loudness


def gaussian(key, extent, width, most, shards=(), kind=jnp.bfloat16):
    values = jax.random.normal(key, extent, jnp.float32) * width
    if len(shards) > 0:
        values = steps_of(key, extent, shards, -0.22, 0.18) * values
    return jnp.clip(values, min=-most, max=most).astype(kind)


def setup_inputs(seed: int = 0) -> dict:
    key_list = jax.random.split(jax.random.key(seed), 10)
    leaf_value = draw_leaf_value(jax.random.fold_in(key_list[9], 71), 0)
    section_cost = draw_section_cost(jax.random.fold_in(key_list[9], 71), 0)
    input_cost = draw_input_cost(jax.random.fold_in(key_list[9], 71), 0)
    dynamics = gaussian(key_list[3], (N, N), N ** -0.5, 0.1875, ((0, 16),), jnp.float32)
    input_map = gaussian(key_list[4], (N, M), N ** -0.5, 0.1875, (), jnp.float32)
    parent_of = draw_parent_of(jax.random.fold_in(key_list[9], 71), 0)
    prob_weight = with_ends(jax.random.randint(key_list[6], (LEAVES,), 1, 17), jax.random.fold_in(key_list[6], 1), 1, 16).astype(jnp.int32)
    parent_state = gaussian(key_list[7], (PARENTS, N), 1.0, 6.0, ((0, 32), (1, 16)), jnp.float32)
    disturbance = gaussian(key_list[8], (LEAVES, N), 1.0, 6.0, ((0, 32), (1, 16)), jnp.float32)
    return dict(leaf_value=leaf_value, section_cost=section_cost, input_cost=input_cost, dynamics=dynamics, input_map=input_map, parent_of=parent_of, prob_weight=prob_weight, parent_state=parent_state, disturbance=disturbance)


highest = lax.Precision.HIGHEST

def reference(leaf_value, section_cost, input_cost, dynamics, input_map, parent_of, prob_weight, parent_state, disturbance):
    weights = prob_weight.astype(jnp.float32)
    labels = jnp.arange(PARENTS, dtype=jnp.int32)
    member = jnp.where(parent_of[None, :] == labels[:, None], weights[None, :], jnp.zeros((), jnp.float32))
    totals = jnp.sum(member, axis=1)

    def per_parent(inputs):
        member_row, parent_total, own_state = inputs
        summed = jnp.einsum('l,lij->ij', member_row, leaf_value, precision=highest)
        expected = summed / parent_total
        propagated = jnp.dot(expected, dynamics, precision=highest)
        curvature = jnp.dot(dynamics.T, propagated, precision=highest)
        coupling = jnp.dot(input_map.T, propagated, precision=highest)
        hessian = input_cost + jnp.dot(input_map.T, jnp.dot(expected, input_map, precision=highest), precision=highest)
        factor = jnp.linalg.cholesky(hessian)
        scaled = lax.linalg.triangular_solve(factor, coupling, left_side=True, lower=True)
        feedback = -lax.linalg.triangular_solve(factor, scaled, left_side=True, lower=True, transpose_a=True)
        new_value = section_cost + curvature - jnp.dot(scaled.T, scaled, precision=highest)
        control = jnp.dot(feedback, own_state, precision=highest)
        following = jnp.dot(dynamics, own_state, precision=highest) + jnp.dot(input_map, control, precision=highest)
        return (new_value, feedback, following)
    new_values, gains, following = lax.map(per_parent, (member, totals, parent_state))
    child_state = following[parent_of] + disturbance
    return (new_values, jnp.swapaxes(gains, 1, 2), child_state)
```

```python
import jax
import jax.numpy as jnp
from jax import lax
from jax.experimental import pallas as pl
from jax.experimental.pallas import tpu as pltpu
from jax.sharding import Mesh, PartitionSpec as P

HI = lax.Precision.HIGHEST
MID = lax.Precision.HIGH
LEAF = ("zh", "y", "c")
MAT = ("x", "zl")
BLK = 64

def _panel_step(q, parents, d_ref, cb_ref):
    lane8 = lax.broadcasted_iota(jnp.int32, (8, 128), 0)
    base = pl.multiple_of(q * 8, 8)
    for p in range(parents):
        for c in range(8):
            cb_ref[p, c] = jnp.broadcast_to(d_ref[p, :, c:c + 1], (BLK, 128))
    rows_of = []
    for p in range(parents):
        def element(r, c):
            return jnp.broadcast_to(cb_ref[p, c, pl.ds(base + r, 1), :], (8, 128))
        low = {}
        inv = []
        rows = []
        for c in range(8):
            pivot = element(c, c)
            for t in range(c):
                pivot = pivot - low[c, t] * low[c, t]
            root = lax.rsqrt(pivot)
            root = root * (1.5 - 0.5 * pivot * root * root)
            inv.append(root)
            for r in range(c + 1, 8):
                value = element(r, c)
                for t in range(c):
                    value = value - low[r, t] * low[c, t]
                low[r, c] = value * root
            line = jnp.broadcast_to(d_ref[p, pl.ds(base + c, 1), :], (8, 128))
            for t in range(c):
                line = line - low[c, t] * rows[t]
            rows.append(line * root)
        back = [None] * 8
        for c in range(7, -1, -1):
            line = rows[c]
            for r in range(7, c, -1):
                line = line - low[r, c] * back[r]
            back[c] = line * inv[c]
        block = rows[0]
        for c in range(1, 8):
            block = jnp.where(lane8 == c, rows[c], block)
        rows_of.append((block, back))
    for p in range(parents):
        block, back = rows_of[p]
        for v in range(BLK // 8):
            old = d_ref[p, v * 8:v * 8 + 8, :]
            new = old
            for c in range(8):
                new = new - cb_ref[p, c, v * 8:v * 8 + 8, :] * back[c]
            new = jnp.where(v > q, new, jnp.where(v == q, block, old))
            d_ref[p, v * 8:v * 8 + 8, :] = pltpu.roll(new, 120, 1)

def factor_kernel(h_ref, out_ref, m_ref, d_ref, cb_ref):
    parents, n, _ = h_ref.shape
    row = lax.broadcasted_iota(jnp.int32, (BLK, 128), 0)
    lane = lax.broadcasted_iota(jnp.int32, (BLK, 128), 1)
    unit = jnp.where(lane == row + BLK, 1.0, 0.0)
    full_r = lax.broadcasted_iota(jnp.int32, (n, n), 0)
    full_c = lax.broadcasted_iota(jnp.int32, (n, n), 1)
    for p in range(parents):
        m_ref[p, :, :n] = h_ref[p]
        m_ref[p, :, n:] = jnp.where(full_r == full_c, 1.0, 0.0)
    for k in range(n // BLK):
        top = k * BLK
        lead = (top // 128) * 128
        stop = n + ((top + BLK + 127) // 128) * 128
        for p in range(parents):
            tile = m_ref[p, top:top + BLK, lead:lead + 128]
            if top != lead:
                tile = pltpu.roll(tile, 128 - (top - lead), 1)
            d_ref[p] = jnp.where(lane < BLK, tile, unit)
        lax.fori_loop(0, BLK // 8, lambda q, _: (_panel_step(q, parents, d_ref, cb_ref), 0)[1], 0)
        for p in range(parents):
            inverse = d_ref[p][:, :BLK]
            scaled = jnp.dot(inverse, m_ref[p, top:top + BLK, lead:stop], precision=HI, preferred_element_type=jnp.float32)
            m_ref[p, top:top + BLK, lead:stop] = scaled
            if top + BLK < n:
                left = jnp.transpose(scaled[:, :n - lead])
                left = left[top + BLK - lead:, :]
                m_ref[p, top + BLK:, lead:stop] = m_ref[p, top + BLK:, lead:stop] - jnp.dot(
                    left, scaled, precision=HI, preferred_element_type=jnp.float32)
    for p in range(parents):
        out_ref[p] = m_ref[p, :, n:]


def inverse_factor(hessian):
    parents, n, _ = hessian.shape
    return pl.pallas_call(
        factor_kernel,
        out_shape=jax.ShapeDtypeStruct(hessian.shape, hessian.dtype),
        scratch_shapes=[
            pltpu.VMEM((parents, n, 2 * n), jnp.float32),
            pltpu.VMEM((parents, BLK, 128), jnp.float32),
            pltpu.VMEM((parents, 8, BLK, 128), jnp.float32),
        ],
        cost_estimate=pl.CostEstimate(flops=10**9, bytes_accessed=10**6, transcendentals=0),
    )(hessian)


def gathered(shard, axis):
    peers = lax.axis_size(axis)
    return lax.all_to_all(jnp.broadcast_to(shard[None], (peers, *shard.shape)), axis, 0, 0, tiled=True)


def ring_gathered(shard, axis):
    up = [(i, (i + 1) % 4) for i in range(4)]
    down = [(b, a) for a, b in up]
    half = shard.shape[0] // 2
    before = lax.ppermute(shard, axis, up)
    after = lax.ppermute(shard, axis, down)
    far_low = lax.ppermute(before[:half], axis, up)
    far_high = lax.ppermute(after[half:], axis, down)
    here = lax.axis_index(axis)
    whole = jnp.zeros((4, *shard.shape), shard.dtype)
    rest = (0,) * (shard.ndim - 1)
    whole = lax.dynamic_update_slice(whole, shard[None], (here, 0, *rest))
    whole = lax.dynamic_update_slice(whole, before[None], ((here + 3) % 4, 0, *rest))
    whole = lax.dynamic_update_slice(whole, after[None], ((here + 1) % 4, 0, *rest))
    whole = lax.dynamic_update_slice(whole, far_low[None], ((here + 2) % 4, 0, *rest))
    return lax.dynamic_update_slice(whole, far_high[None], ((here + 2) % 4, half, *rest))


def neighbours(low_out, high_out):
    count = lax.axis_size(LEAF)
    forward = [(i, i + 1) for i in range(count - 1)]
    backward = [(b, a) for a, b in forward]
    return lax.ppermute(high_out, LEAF, forward), lax.ppermute(low_out, LEAF, backward)


def local(
    leaf_value,
    section_cost,
    input_cost,
    dynamics,
    input_map,
    parent_of,
    prob_weight,
    parent_state,
    disturbance,
):
    leaf_dev, slab, states = leaf_value.shape
    par_dev = parent_state.shape[0]
    inputs = input_map.shape[1]
    leaf_index = lax.axis_index(LEAF)
    column = lax.axis_index(MAT)
    core = lax.axis_index("c")
    row_start = column * slab

    piece = lax.dynamic_slice_in_dim(dynamics, (core * 4 + lax.axis_index("y")) * 128, 128, 1)
    state_rows = jnp.pad(parent_state, ((0, 8 - par_dev), (0, 128 - slab)))
    from_mat = gathered(jnp.concatenate([piece, state_rows], axis=0), MAT)
    state = jnp.moveaxis(from_mat[:, slab : slab + par_dev, :slab], 0, 1).reshape(par_dev, states)
    half_dyn = gathered(from_mat[:, :slab].reshape(states, 128), "y")
    other_dyn = lax.ppermute(half_dyn, "c", [(0, 1), (1, 0)])
    pieces = jnp.zeros((8, states, 128), jnp.float32)
    pieces = lax.dynamic_update_slice(pieces, half_dyn, (core * 4, 0, 0))
    pieces = lax.dynamic_update_slice(pieces, other_dyn, (4 - core * 4, 0, 0))
    full_dyn = jnp.moveaxis(pieces, 0, 1).reshape(states, states)

    weights = prob_weight.astype(jnp.float32)
    my_parents = lax.dynamic_slice_in_dim(parent_of, leaf_index * leaf_dev, leaf_dev, 0)
    my_weights = lax.dynamic_slice_in_dim(weights, leaf_index * leaf_dev, leaf_dev, 0)
    first_label = leaf_index * par_dev
    slot_ids = jnp.arange(par_dev + 2, dtype=jnp.int32)
    chosen = (my_parents - first_label + 1)[:, None] == slot_ids[None, :]
    member = jnp.where(chosen, my_weights[:, None], 0.0)
    labels = first_label + jnp.arange(par_dev, dtype=jnp.int32)
    totals = jnp.sum(
        jnp.where(parent_of[:, None] == labels[None, :], weights[:, None], 0.0), axis=0
    )
    terms = jnp.einsum("st,sij->tij", member, leaf_value, precision=HI)
    from_low, from_high = neighbours(terms[0], terms[par_dev + 1])
    expected = [(terms[1] + from_low) / totals[0], (terms[2] + from_high) / totals[1]]
    input_side = jnp.concatenate([jnp.dot(e, input_map, precision=HI) for e in expected], axis=1)

    line = gathered(input_side, "zl").reshape(4 * slab, par_dev * inputs)
    input_full = ring_gathered(line, "x").reshape(states, par_dev * inputs)
    both = lax.dot_general(input_map, input_full, (((0,), (0,)), ((), ())), precision=HI)
    hessian = jnp.stack([input_cost + both[:, p * inputs : (p + 1) * inputs] for p in range(par_dev)])
    inverse = inverse_factor(hessian)

    stacked = jnp.concatenate(expected, axis=0)
    turned = lax.dot_general(full_dyn, stacked, (((0,), (1,)), ((), ())), precision=MID)
    arrived = lax.all_to_all(turned.reshape(states // slab, slab, par_dev * slab), MAT, 0, 0, tiled=True)
    columns = arrived.reshape(states // slab, slab, par_dev, slab).transpose(2, 1, 0, 3)
    columns = columns.reshape(par_dev * slab, states)
    curvature = jnp.dot(columns, full_dyn, precision=MID).reshape(par_dev, slab, states)
    coupling_rows = jnp.dot(columns, input_map, precision=HI).reshape(par_dev, slab, inputs)
    coupling = lax.dot_general(input_full, full_dyn, (((0,), (0,)), ((), ())), precision=MID)
    coupling = coupling.reshape(par_dev, inputs, states)

    scaled_rows = jnp.einsum("pja,pba->pjb", coupling_rows, inverse, precision=HI)
    gain_rows = -jnp.einsum("pjb,pba->pja", scaled_rows, inverse, precision=HI)
    new_value = section_cost[None] + curvature + jnp.einsum("pja,pan->pjn", gain_rows, coupling, precision=MID)

    coupled_state = jnp.einsum("pan,pn->pa", coupling, state, precision=HI)
    control = -jnp.einsum("pba,pb->pa", inverse, jnp.einsum("pba,pa->pb", inverse, coupled_state, precision=HI), precision=HI)
    input_rows = lax.dynamic_slice_in_dim(input_map, row_start, slab, 0)
    following = jnp.einsum("ij,pj->pi", dynamics, state, precision=HI) + jnp.einsum(
        "ia,pa->pi", input_rows, control, precision=HI
    )
    below, above = neighbours(following[:1], following[par_dev - 1 :])
    extended = jnp.concatenate([below, following, above], axis=0)
    child_state = jnp.einsum("st,tj->sj", chosen.astype(jnp.float32), extended, precision=HI) + disturbance
    return (new_value, gain_rows, child_state)


def solution(mesh):
    fine = Mesh(mesh.devices.reshape(4, 4, 2, 4, 4), (*LEAF, *MAT))
    in_specs = (
        P(LEAF, MAT, None),
        P(MAT, None),
        P(),
        P(MAT, None),
        P(),
        P(),
        P(),
        P(LEAF, MAT),
        P(LEAF, MAT),
    )
    out_specs = (P(LEAF, MAT, None), P(LEAF, MAT, None), P(LEAF, MAT))
    return jax.shard_map(local, mesh=fine, in_specs=in_specs, out_specs=out_specs, check_vma=False)
```

```python
import jax
import jax.numpy as jnp
from jax import lax
from jax.experimental import pallas as pl
from jax.experimental.pallas import tpu as pltpu
from jax.sharding import Mesh, PartitionSpec as P

HI = lax.Precision.HIGHEST
LEAF = ("zh", "y", "c")
MAT = ("x", "zl")
BLK = 64


def _panel_step(q, parents, d_ref, cb_ref):
    lane8 = lax.broadcasted_iota(jnp.int32, (8, 128), 0)
    base = pl.multiple_of(q * 8, 8)
    for p in range(parents):
        for c in range(8):
            cb_ref[p, c] = jnp.broadcast_to(d_ref[p, :, c:c + 1], (BLK, 128))
    rows_of = []
    for p in range(parents):
        def element(r, c):
            return jnp.broadcast_to(cb_ref[p, c, pl.ds(base + r, 1), :], (8, 128))

        low = {}
        inv = []
        rows = []
        for c in range(8):
            pivot = element(c, c)
            for t in range(c):
                pivot = pivot - low[c, t] * low[c, t]
            root = lax.rsqrt(pivot)
            root = root * (1.5 - 0.5 * pivot * root * root)
            inv.append(root)
            for r in range(c + 1, 8):
                value = element(r, c)
                for t in range(c):
                    value = value - low[r, t] * low[c, t]
                low[r, c] = value * root
            line = jnp.broadcast_to(d_ref[p, pl.ds(base + c, 1), :], (8, 128))
            for t in range(c):
                line = line - low[c, t] * rows[t]
            rows.append(line * root)
        back = [None] * 8
        for c in range(7, -1, -1):
            line = rows[c]
            for r in range(7, c, -1):
                line = line - low[r, c] * back[r]
            back[c] = line * inv[c]
        block = rows[0]
        for c in range(1, 8):
            block = jnp.where(lane8 == c, rows[c], block)
        rows_of.append((block, back))
    for p in range(parents):
        block, back = rows_of[p]
        for v in range(BLK // 8):
            old = d_ref[p, v * 8:v * 8 + 8, :]
            new = old
            for c in range(8):
                new = new - cb_ref[p, c, v * 8:v * 8 + 8, :] * back[c]
            new = jnp.where(v > q, new, jnp.where(v == q, block, old))
            d_ref[p, v * 8:v * 8 + 8, :] = pltpu.roll(new, 120, 1)


def factor_kernel(h_ref, out_ref, m_ref, d_ref, cb_ref):
    parents, n, _ = h_ref.shape
    row = lax.broadcasted_iota(jnp.int32, (BLK, 128), 0)
    lane = lax.broadcasted_iota(jnp.int32, (BLK, 128), 1)
    unit = jnp.where(lane == row + BLK, 1.0, 0.0)
    full_r = lax.broadcasted_iota(jnp.int32, (n, n), 0)
    full_c = lax.broadcasted_iota(jnp.int32, (n, n), 1)
    for p in range(parents):
        m_ref[p, :, :n] = h_ref[p]
        m_ref[p, :, n:] = jnp.where(full_r == full_c, 1.0, 0.0)
    for k in range(n // BLK):
        top = k * BLK
        lead = (top // 128) * 128
        stop = n + ((top + BLK + 127) // 128) * 128
        for p in range(parents):
            tile = m_ref[p, top:top + BLK, lead:lead + 128]
            if top != lead:
                tile = pltpu.roll(tile, 128 - (top - lead), 1)
            d_ref[p] = jnp.where(lane < BLK, tile, unit)
        lax.fori_loop(0, BLK // 8, lambda q, _: (_panel_step(q, parents, d_ref, cb_ref), 0)[1], 0)
        for p in range(parents):
            inverse = d_ref[p][:, :BLK]
            scaled = jnp.dot(inverse, m_ref[p, top:top + BLK, lead:stop], precision=HI, preferred_element_type=jnp.float32)
            m_ref[p, top:top + BLK, lead:stop] = scaled
            if top + BLK < n:
                left = jnp.transpose(scaled[:, :n - lead])
                left = left[top + BLK - lead:, :]
                m_ref[p, top + BLK:, lead:stop] = m_ref[p, top + BLK:, lead:stop] - jnp.dot(
                    left, scaled, precision=HI, preferred_element_type=jnp.float32)
    for p in range(parents):
        out_ref[p] = m_ref[p, :, n:]


def split(value):
    high = value.astype(jnp.bfloat16)
    return high, (value - high.astype(jnp.float32)).astype(jnp.bfloat16)


def three_pass(left, right, dims=(((1,), (0,)), ((), ()))):
    def part(a, b):
        return lax.dot_general(a, b, dims, preferred_element_type=jnp.float32)

    return part(left[0], right[1]) + part(left[1], right[0]) + part(left[0], right[0])


def exact(left, right, dims=(((1,), (0,)), ((), ()))):
    return lax.dot_general(left, right, dims, precision=HI, preferred_element_type=jnp.float32)


CROSS = (((1,), (1,)), ((), ()))


def piece_of(step, core):
    return jnp.where(step < 4, core * 4 + step, (1 - core) * 4 + step - 4)


def transition_kernel(core_ref, own_ref, other_ref, value_ref, state_ref, turned_ref, high_ref, low_ref, drift_ref, vh_ref, vl_ref, acc_ref):
    step = pl.program_id(0)
    states = value_ref.shape[1]

    @pl.when(step == 0)
    def _():
        vh_ref[...], vl_ref[...] = split(value_ref[...])
        acc_ref[...] = jnp.zeros_like(acc_ref)

    piece = jnp.where(step < 4, own_ref[0, :, :64, :], other_ref[0, :, :64, :]).reshape(states, 128)
    high, low = split(piece)
    high_ref[...] = high
    low_ref[...] = low
    turned_ref[...] = jnp.transpose(three_pass((vh_ref[...], vl_ref[...]), (high, low)))
    for p in range(2):
        acc_ref[p] = acc_ref[p] + piece * state_ref[p : p + 1, :]

    @pl.when(step == 7)
    def _():
        for p in range(2):
            drift_ref[p] = jnp.broadcast_to(jnp.sum(acc_ref[p], axis=1, keepdims=True), (states, 128))


def transition_products(core, own, other, value, state):
    states = value.shape[1]
    rows = own.shape[1:]
    grid = pltpu.PrefetchScalarGridSpec(
        num_scalar_prefetch=1,
        grid=(8,),
        in_specs=[
            pl.BlockSpec((1, *rows), lambda s, c: (jnp.minimum(s, 3), 0, 0, 0)),
            pl.BlockSpec((1, *rows), lambda s, c: (jnp.maximum(s - 4, 0), 0, 0, 0)),
            pl.BlockSpec(value.shape, lambda s, c: (0, 0)),
            pl.BlockSpec((8, 128), lambda s, c: (0, piece_of(s, c[0]))),
        ],
        out_specs=[
            pl.BlockSpec((128, 128), lambda s, c: (piece_of(s, c[0]), 0)),
            pl.BlockSpec((states, 128), lambda s, c: (0, piece_of(s, c[0]))),
            pl.BlockSpec((states, 128), lambda s, c: (0, piece_of(s, c[0]))),
            pl.BlockSpec((2, states, 128), lambda s, c: (0, 0, 0)),
        ],
        scratch_shapes=[
            pltpu.VMEM(value.shape, jnp.bfloat16),
            pltpu.VMEM(value.shape, jnp.bfloat16),
            pltpu.VMEM((2, states, 128), jnp.float32),
        ],
    )
    return pl.pallas_call(
        transition_kernel,
        grid_spec=grid,
        out_shape=[
            jax.ShapeDtypeStruct((states, 128), jnp.float32),
            jax.ShapeDtypeStruct((states, states), jnp.bfloat16),
            jax.ShapeDtypeStruct((states, states), jnp.bfloat16),
            jax.ShapeDtypeStruct((2, states, 128), jnp.float32),
        ],
        cost_estimate=pl.CostEstimate(flops=10**9, bytes_accessed=14 * 10**6, transcendentals=0),
    )(core, own, other, value, state)


def blocks_of(slot_ref, line_refs):
    own, before, after, far_low, far_high = line_refs
    slot = slot_ref[0]

    def start(offset):
        return pl.multiple_of(((slot + offset) & 3) * 256, 256)

    return [(start(0), own), (start(3), before), (start(1), after), (start(2), far_low), (start(2) + 128, far_high)]


def hessian_kernel(slot_ref, turned_map_ref, cost_ref, drift_ref, own, before, after, far_low, far_high, out_ref, control_ref, h_ref, m_ref, d_ref, cb_ref):
    n = cost_ref.shape[0]
    parents = out_ref.shape[0]
    total = None
    pull = [jnp.zeros((8, n), jnp.float32) for _ in range(parents)]
    for start, ref in blocks_of(slot_ref, (own, before, after, far_low, far_high)):
        rows = ref.shape[0]
        start = pl.multiple_of(start, 128)
        term = exact(turned_map_ref[:, pl.ds(start, rows)], ref[...])
        total = term if total is None else total + term
        for p in range(parents):
            weight = drift_ref[p, pl.ds(start, rows), :]
            product = ref[:, p * n : (p + 1) * n] * jnp.concatenate([weight] * (n // 128), axis=1)
            pull[p] = pull[p] + jnp.sum(product.reshape(rows // 8, 8, n), axis=0)
    for p in range(parents):
        h_ref[p] = cost_ref[...] + total[:, p * n : (p + 1) * n]
    factor_kernel(h_ref, out_ref, m_ref, d_ref, cb_ref)
    for p in range(parents):
        coupled = jnp.broadcast_to(jnp.sum(pull[p], axis=0, keepdims=True), (8, n))
        control_ref[p] = -exact(exact(coupled, out_ref[p], CROSS), out_ref[p])


def factor_and_control(slot, turned_map, cost, drift, lines, parents):
    n = cost.shape[0]
    vmem = pl.BlockSpec(memory_space=pltpu.VMEM)
    return pl.pallas_call(
        hessian_kernel,
        in_specs=[pl.BlockSpec(memory_space=pltpu.SMEM)] + [vmem] * 8,
        out_specs=[vmem] * 2,
        out_shape=[
            jax.ShapeDtypeStruct((parents, n, n), jnp.float32),
            jax.ShapeDtypeStruct((parents, 8, n), jnp.float32),
        ],
        scratch_shapes=[
            pltpu.VMEM((parents, n, n), jnp.float32),
            pltpu.VMEM((parents, n, 2 * n), jnp.float32),
            pltpu.VMEM((parents, BLK, 128), jnp.float32),
            pltpu.VMEM((parents, 8, BLK, 128), jnp.float32),
        ],
        cost_estimate=pl.CostEstimate(flops=10**10, bytes_accessed=4 * 10**6, transcendentals=0),
    )(slot, turned_map, cost, drift, *lines)


def value_kernel(slot_ref, arrived_ref, map_ref, inverse_ref, own, before, after, far_low, far_high, high_ref, low_ref, section_ref, value_ref, gain_ref, cols_ref):
    parents, slab, n = gain_ref.shape
    states = section_ref.shape[1]
    lane = lax.broadcasted_iota(jnp.int32, (slab, 128), 1)
    for i in range(states // 128):
        even, odd = arrived_ref[2 * i], arrived_ref[2 * i + 1]
        cols_ref[:slab, i * 128 : (i + 1) * 128] = jnp.where(lane < 64, even, pltpu.roll(odd, 64, 1))
        cols_ref[slab:, i * 128 : (i + 1) * 128] = jnp.where(lane < 64, pltpu.roll(even, 64, 1), odd)
    coupling = exact(cols_ref[...], map_ref[...])
    for p in range(parents):
        rows = slice(p * slab, (p + 1) * slab)
        gain = -exact(exact(coupling[rows], inverse_ref[p], CROSS), inverse_ref[p])
        gain_ref[p] = gain
        for start, ref in blocks_of(slot_ref, (own, before, after, far_low, far_high)):
            count = ref.shape[0]
            start = pl.multiple_of(start, 128)
            change = exact(gain, ref[:, p * n : (p + 1) * n], CROSS)
            cols_ref[rows, pl.ds(start, count)] = cols_ref[rows, pl.ds(start, count)] + change
    left = split(cols_ref[...])
    for j in range(states // 256):
        span = slice(j * 256, (j + 1) * 256)
        part = three_pass(left, (high_ref[:, span], low_ref[:, span]))
        for p in range(parents):
            value_ref[p, :, span] = section_ref[:, span] + part[p * slab : (p + 1) * slab]


def value_and_gain(slot, arrived, input_map, inverse, lines, high, low, section):
    parents, n, _ = inverse.shape
    slab, states = section.shape
    vmem = pl.BlockSpec(memory_space=pltpu.VMEM)
    return pl.pallas_call(
        value_kernel,
        in_specs=[pl.BlockSpec(memory_space=pltpu.SMEM)] + [vmem] * 11,
        out_specs=[vmem] * 2,
        out_shape=[
            jax.ShapeDtypeStruct((parents, slab, states), jnp.float32),
            jax.ShapeDtypeStruct((parents, slab, n), jnp.float32),
        ],
        scratch_shapes=[pltpu.VMEM((parents * slab, states), jnp.float32)],
        cost_estimate=pl.CostEstimate(flops=3 * 10**9, bytes_accessed=8 * 10**6, transcendentals=0),
    )(slot, arrived, input_map, inverse, *lines, high, low, section)


def gathered(shard, axis):
    peers = lax.axis_size(axis)
    return lax.all_to_all(jnp.broadcast_to(shard[None], (peers, *shard.shape)), axis, 0, 0, tiled=True)


def ring_parts(shard, axis):
    up = [(i, (i + 1) % 4) for i in range(4)]
    down = [(b, a) for a, b in up]
    half = shard.shape[0] // 2
    before = lax.ppermute(shard, axis, up)
    after = lax.ppermute(shard, axis, down)
    far_low = lax.ppermute(before[:half], axis, up)
    far_high = lax.ppermute(after[half:], axis, down)
    return shard, before, after, far_low, far_high


def neighbours(low_out, high_out):
    count = lax.axis_size(LEAF)
    forward = [(i, i + 1) for i in range(count - 1)]
    backward = [(b, a) for a, b in forward]
    return lax.ppermute(high_out, LEAF, forward), lax.ppermute(low_out, LEAF, backward)


def local(
    leaf_value,
    section_cost,
    input_cost,
    dynamics,
    input_map,
    parent_of,
    prob_weight,
    parent_state,
    disturbance,
):
    leaf_dev, slab, states = leaf_value.shape
    par_dev = parent_state.shape[0]
    inputs = input_map.shape[1]
    leaf_index = lax.axis_index(LEAF)
    column = lax.axis_index(MAT)
    core = lax.axis_index("c")
    slot = lax.axis_index("x").astype(jnp.int32)[None]
    row_start = column * slab

    piece = lax.dynamic_slice_in_dim(dynamics, (core * 4 + lax.axis_index("y")) * 128, 128, 1)
    state_rows = jnp.pad(parent_state, ((0, 8 - par_dev), (0, 128 - slab)))
    from_mat = gathered(jnp.concatenate([piece, state_rows], axis=0), MAT)
    state = jnp.moveaxis(from_mat[:, slab : slab + par_dev, :slab], 0, 1).reshape(par_dev, states)

    weights = prob_weight.astype(jnp.float32)
    my_parents = lax.dynamic_slice_in_dim(parent_of, leaf_index * leaf_dev, leaf_dev, 0)
    my_weights = lax.dynamic_slice_in_dim(weights, leaf_index * leaf_dev, leaf_dev, 0)
    first_label = leaf_index * par_dev
    slot_ids = jnp.arange(par_dev + 2, dtype=jnp.int32)
    chosen = (my_parents - first_label + 1)[:, None] == slot_ids[None, :]
    member = jnp.where(chosen, my_weights[:, None], 0.0)
    labels = first_label + jnp.arange(par_dev, dtype=jnp.int32)
    totals = jnp.sum(
        jnp.where(parent_of[:, None] == labels[None, :], weights[:, None], 0.0), axis=0
    )
    terms = jnp.einsum("st,sij->tij", member, leaf_value, precision=HI)
    mapped = jnp.dot(terms.reshape(-1, states), input_map, precision=HI).reshape(par_dev + 2, slab, inputs)
    map_low, map_high = lax.optimization_barrier(neighbours(mapped[0], mapped[par_dev + 1]))
    from_low, from_high = lax.optimization_barrier(neighbours(terms[0], terms[par_dev + 1]))
    input_side = jnp.concatenate([(mapped[1] + map_low) / totals[0], (mapped[2] + map_high) / totals[1]], axis=1)

    line = gathered(input_side, "zl").reshape(4 * slab, par_dev * inputs)
    lines = ring_parts(line, "x")

    own_dyn = gathered(from_mat, "y")
    other_dyn = lax.ppermute(own_dyn, "c", [(0, 1), (1, 0)])
    expected = jnp.concatenate([(terms[1] + from_low) / totals[0], (terms[2] + from_high) / totals[1]], axis=0)
    turned, high, low, drift = transition_products(
        core.astype(jnp.int32)[None], own_dyn, other_dyn, expected, jnp.pad(state, ((0, 8 - par_dev), (0, 0)))
    )
    arrived = lax.all_to_all(turned.reshape(states // slab, slab, par_dev * slab), MAT, 0, 0, tiled=True)
    inverse, control = factor_and_control(slot, input_map.T, input_cost, drift, lines, par_dev)

    input_rows = lax.dynamic_slice_in_dim(input_map, row_start, slab, 0)
    following = jnp.einsum("ij,pj->pi", dynamics, state, precision=HI) + jnp.einsum(
        "ia,pa->pi", input_rows, control[:, 0], precision=HI
    )
    below, above = neighbours(following[:1], following[par_dev - 1 :])
    new_value, gain_rows = value_and_gain(slot, arrived, input_map, inverse, lines, high, low, section_cost)
    below, above, new_value = lax.optimization_barrier((below, above, new_value))
    extended = jnp.concatenate([below, following, above], axis=0)
    child_state = jnp.einsum("st,tj->sj", chosen.astype(jnp.float32), extended, precision=HI) + disturbance
    return (new_value, gain_rows, child_state)


def solution(mesh):
    fine = Mesh(mesh.devices.reshape(4, 4, 2, 4, 4), (*LEAF, *MAT))
    in_specs = (
        P(LEAF, MAT, None),
        P(MAT, None),
        P(),
        P(MAT, None),
        P(),
        P(),
        P(),
        P(LEAF, MAT),
        P(LEAF, MAT),
    )
    out_specs = (P(LEAF, MAT, None), P(LEAF, MAT, None), P(LEAF, MAT))
    return jax.shard_map(local, mesh=fine, in_specs=in_specs, out_specs=out_specs, check_vma=False)
```

```python
import jax
import jax.numpy as jnp
from jax import lax
from jax.experimental import pallas as pl
from jax.experimental.pallas import tpu as pltpu
from jax.sharding import Mesh, PartitionSpec as P

HI = lax.Precision.HIGHEST
LEAF = ("zh", "y", "c")
MAT = ("x", "zl")
BLK = 64


def _panel_step(q, parents, d_ref, cb_ref):
    lane8 = lax.broadcasted_iota(jnp.int32, (8, 128), 0)
    base = pl.multiple_of(q * 8, 8)
    for p in range(parents):
        for c in range(8):
            cb_ref[p, c] = jnp.broadcast_to(d_ref[p, :, c:c + 1], (BLK, 128))
    rows_of = []
    for p in range(parents):
        def element(r, c):
            return jnp.broadcast_to(cb_ref[p, c, pl.ds(base + r, 1), :], (8, 128))

        low = {}
        inv = []
        rows = []
        for c in range(8):
            pivot = element(c, c)
            for t in range(c):
                pivot = pivot - low[c, t] * low[c, t]
            root = lax.rsqrt(pivot)
            root = root * (1.5 - 0.5 * pivot * root * root)
            inv.append(root)
            for r in range(c + 1, 8):
                value = element(r, c)
                for t in range(c):
                    value = value - low[r, t] * low[c, t]
                low[r, c] = value * root
            line = jnp.broadcast_to(d_ref[p, pl.ds(base + c, 1), :], (8, 128))
            for t in range(c):
                line = line - low[c, t] * rows[t]
            rows.append(line * root)
        back = [None] * 8
        for c in range(7, -1, -1):
            line = rows[c]
            for r in range(7, c, -1):
                line = line - low[r, c] * back[r]
            back[c] = line * inv[c]
        block = rows[0]
        for c in range(1, 8):
            block = jnp.where(lane8 == c, rows[c], block)
        rows_of.append((block, back))
    for p in range(parents):
        block, back = rows_of[p]
        for v in range(BLK // 8):
            old = d_ref[p, v * 8:v * 8 + 8, :]
            new = old
            for c in range(8):
                new = new - cb_ref[p, c, v * 8:v * 8 + 8, :] * back[c]
            new = jnp.where(v > q, new, jnp.where(v == q, block, old))
            d_ref[p, v * 8:v * 8 + 8, :] = pltpu.roll(new, 120, 1)


def factor_kernel(h_ref, out_ref, m_ref, d_ref, cb_ref):
    parents, n, _ = h_ref.shape
    row = lax.broadcasted_iota(jnp.int32, (BLK, 128), 0)
    lane = lax.broadcasted_iota(jnp.int32, (BLK, 128), 1)
    unit = jnp.where(lane == row + BLK, 1.0, 0.0)
    full_r = lax.broadcasted_iota(jnp.int32, (n, n), 0)
    full_c = lax.broadcasted_iota(jnp.int32, (n, n), 1)
    for p in range(parents):
        m_ref[p, :, :n] = h_ref[p]
        m_ref[p, :, n:] = jnp.where(full_r == full_c, 1.0, 0.0)
    for k in range(n // BLK):
        top = k * BLK
        lead = (top // 128) * 128
        stop = n + ((top + BLK + 127) // 128) * 128
        for p in range(parents):
            tile = m_ref[p, top:top + BLK, lead:lead + 128]
            if top != lead:
                tile = pltpu.roll(tile, 128 - (top - lead), 1)
            d_ref[p] = jnp.where(lane < BLK, tile, unit)
        lax.fori_loop(0, BLK // 8, lambda q, _: (_panel_step(q, parents, d_ref, cb_ref), 0)[1], 0)
        for p in range(parents):
            inverse = d_ref[p][:, :BLK]
            scaled = jnp.dot(inverse, m_ref[p, top:top + BLK, lead:stop], precision=HI, preferred_element_type=jnp.float32)
            m_ref[p, top:top + BLK, lead:stop] = scaled
            if top + BLK < n:
                left = jnp.transpose(scaled[:, :n - lead])
                left = left[top + BLK - lead:, :]
                m_ref[p, top + BLK:, lead:stop] = m_ref[p, top + BLK:, lead:stop] - jnp.dot(
                    left, scaled, precision=HI, preferred_element_type=jnp.float32)
    for p in range(parents):
        out_ref[p] = m_ref[p, :, n:]


def split(value):
    high = value.astype(jnp.bfloat16)
    return high, (value - high.astype(jnp.float32)).astype(jnp.bfloat16)


def three_pass(left, right, dims=(((1,), (0,)), ((), ()))):
    def part(a, b):
        return lax.dot_general(a, b, dims, preferred_element_type=jnp.float32)

    return part(left[0], right[1]) + part(left[1], right[0]) + part(left[0], right[0])


def exact(left, right, dims=(((1,), (0,)), ((), ()))):
    return lax.dot_general(left, right, dims, precision=HI, preferred_element_type=jnp.float32)


CROSS = (((1,), (1,)), ((), ()))


def piece_of(step, core):
    return jnp.where(step < 4, core * 4 + step, (1 - core) * 4 + step - 4)


def transition_kernel(core_ref, own_ref, other_ref, value_ref, state_ref, turned_ref, high_ref, low_ref, drift_ref, vh_ref, vl_ref, acc_ref):
    step = pl.program_id(0)
    states = value_ref.shape[1]

    @pl.when(step == 0)
    def _():
        vh_ref[...], vl_ref[...] = split(value_ref[...])
        acc_ref[...] = jnp.zeros_like(acc_ref)

    piece = jnp.where(step < 4, own_ref[0, :, :64, :], other_ref[0, :, :64, :]).reshape(states, 128)
    high, low = split(piece)
    high_ref[...] = high
    low_ref[...] = low
    turned_ref[...] = jnp.transpose(three_pass((vh_ref[...], vl_ref[...]), (high, low)))
    for p in range(2):
        acc_ref[p] = acc_ref[p] + piece * state_ref[p : p + 1, :]

    @pl.when(step == 7)
    def _():
        for p in range(2):
            drift_ref[p] = jnp.broadcast_to(jnp.sum(acc_ref[p], axis=1, keepdims=True), (states, 128))


def transition_products(core, own, other, value, state):
    states = value.shape[1]
    rows = own.shape[1:]
    grid = pltpu.PrefetchScalarGridSpec(
        num_scalar_prefetch=1,
        grid=(8,),
        in_specs=[
            pl.BlockSpec((1, *rows), lambda s, c: (jnp.minimum(s, 3), 0, 0, 0)),
            pl.BlockSpec((1, *rows), lambda s, c: (jnp.maximum(s - 4, 0), 0, 0, 0)),
            pl.BlockSpec(value.shape, lambda s, c: (0, 0)),
            pl.BlockSpec((8, 128), lambda s, c: (0, piece_of(s, c[0]))),
        ],
        out_specs=[
            pl.BlockSpec((128, 128), lambda s, c: (piece_of(s, c[0]), 0)),
            pl.BlockSpec((states, 128), lambda s, c: (0, piece_of(s, c[0]))),
            pl.BlockSpec((states, 128), lambda s, c: (0, piece_of(s, c[0]))),
            pl.BlockSpec((2, states, 128), lambda s, c: (0, 0, 0)),
        ],
        scratch_shapes=[
            pltpu.VMEM(value.shape, jnp.bfloat16),
            pltpu.VMEM(value.shape, jnp.bfloat16),
            pltpu.VMEM((2, states, 128), jnp.float32),
        ],
    )
    return pl.pallas_call(
        transition_kernel,
        grid_spec=grid,
        out_shape=[
            jax.ShapeDtypeStruct((states, 128), jnp.float32),
            jax.ShapeDtypeStruct((states, states), jnp.bfloat16),
            jax.ShapeDtypeStruct((states, states), jnp.bfloat16),
            jax.ShapeDtypeStruct((2, states, 128), jnp.float32),
        ],
        cost_estimate=pl.CostEstimate(flops=10**9, bytes_accessed=14 * 10**6, transcendentals=0),
    )(core, own, other, value, state)


def blocks_of(slot_ref, line_refs):
    return [(pl.multiple_of((slot_ref[0] ^ k) * 256, 256), ref) for k, ref in enumerate(line_refs)]


def hessian_kernel(slot_ref, turned_map_ref, cost_ref, drift_ref, line0, line1, line2, line3, out_ref, control_ref, h_ref, m_ref, d_ref, cb_ref):
    n = cost_ref.shape[0]
    parents = out_ref.shape[0]
    total = None
    pull = [jnp.zeros((8, n), jnp.float32) for _ in range(parents)]
    for start, ref in blocks_of(slot_ref, (line0, line1, line2, line3)):
        rows = ref.shape[0]
        term = exact(turned_map_ref[:, pl.ds(start, rows)], ref[...])
        total = term if total is None else total + term
        for p in range(parents):
            weight = drift_ref[p, pl.ds(start, rows), :]
            product = ref[:, p * n : (p + 1) * n] * jnp.concatenate([weight] * (n // 128), axis=1)
            pull[p] = pull[p] + jnp.sum(product.reshape(rows // 8, 8, n), axis=0)
    for p in range(parents):
        h_ref[p] = cost_ref[...] + total[:, p * n : (p + 1) * n]
    factor_kernel(h_ref, out_ref, m_ref, d_ref, cb_ref)
    for p in range(parents):
        coupled = jnp.broadcast_to(jnp.sum(pull[p], axis=0, keepdims=True), (8, n))
        control_ref[p] = -exact(exact(coupled, out_ref[p], CROSS), out_ref[p])


def factor_and_control(slot, turned_map, cost, drift, lines, parents):
    n = cost.shape[0]
    vmem = pl.BlockSpec(memory_space=pltpu.VMEM)
    return pl.pallas_call(
        hessian_kernel,
        in_specs=[pl.BlockSpec(memory_space=pltpu.SMEM)] + [vmem] * 7,
        out_specs=[vmem] * 2,
        out_shape=[
            jax.ShapeDtypeStruct((parents, n, n), jnp.float32),
            jax.ShapeDtypeStruct((parents, 8, n), jnp.float32),
        ],
        scratch_shapes=[
            pltpu.VMEM((parents, n, n), jnp.float32),
            pltpu.VMEM((parents, n, 2 * n), jnp.float32),
            pltpu.VMEM((parents, BLK, 128), jnp.float32),
            pltpu.VMEM((parents, 8, BLK, 128), jnp.float32),
        ],
        cost_estimate=pl.CostEstimate(flops=10**10, bytes_accessed=4 * 10**6, transcendentals=0),
    )(slot, turned_map, cost, drift, *lines)


def value_kernel(slot_ref, arrived_ref, map_ref, inverse_ref, line0, line1, line2, line3, high_ref, low_ref, section_ref, value_ref, gain_ref, cols_ref):
    parents, slab, n = gain_ref.shape
    states = section_ref.shape[1]
    lane = lax.broadcasted_iota(jnp.int32, (slab, 128), 1)
    for i in range(states // 128):
        even, odd = arrived_ref[2 * i], arrived_ref[2 * i + 1]
        cols_ref[:slab, i * 128 : (i + 1) * 128] = jnp.where(lane < 64, even, pltpu.roll(odd, 64, 1))
        cols_ref[slab:, i * 128 : (i + 1) * 128] = jnp.where(lane < 64, pltpu.roll(even, 64, 1), odd)
    coupling = exact(cols_ref[...], map_ref[...])
    for p in range(parents):
        rows = slice(p * slab, (p + 1) * slab)
        gain = -exact(exact(coupling[rows], inverse_ref[p], CROSS), inverse_ref[p])
        gain_ref[p] = gain
        for start, ref in blocks_of(slot_ref, (line0, line1, line2, line3)):
            count = ref.shape[0]
            change = exact(gain, ref[:, p * n : (p + 1) * n], CROSS)
            cols_ref[rows, pl.ds(start, count)] = cols_ref[rows, pl.ds(start, count)] + change
    left = split(cols_ref[...])
    for j in range(states // 256):
        span = slice(j * 256, (j + 1) * 256)
        part = three_pass(left, (high_ref[:, span], low_ref[:, span]))
        for p in range(parents):
            value_ref[p, :, span] = section_ref[:, span] + part[p * slab : (p + 1) * slab]


def value_and_gain(slot, arrived, input_map, inverse, lines, high, low, section):
    parents, n, _ = inverse.shape
    slab, states = section.shape
    vmem = pl.BlockSpec(memory_space=pltpu.VMEM)
    return pl.pallas_call(
        value_kernel,
        in_specs=[pl.BlockSpec(memory_space=pltpu.SMEM)] + [vmem] * 10,
        out_specs=[vmem] * 2,
        out_shape=[
            jax.ShapeDtypeStruct((parents, slab, states), jnp.float32),
            jax.ShapeDtypeStruct((parents, slab, n), jnp.float32),
        ],
        scratch_shapes=[pltpu.VMEM((parents * slab, states), jnp.float32)],
        cost_estimate=pl.CostEstimate(flops=3 * 10**9, bytes_accessed=8 * 10**6, transcendentals=0),
    )(slot, arrived, input_map, inverse, *lines, high, low, section)


def gathered(shard, axis):
    peers = lax.axis_size(axis)
    return lax.all_to_all(jnp.broadcast_to(shard[None], (peers, *shard.shape)), axis, 0, 0, tiled=True)


def sent(value, axis, pairs):
    return lax.ppermute(value, axis, pairs)


def exchanged(shard, axis):
    return [shard] + [sent(shard, axis, [(i, i ^ k) for i in range(4)]) for k in (1, 2, 3)]


def in_order(blocks, place):
    rows = []
    for k in range(4):
        value = blocks[3]
        for distance in (2, 1, 0):
            value = jnp.where(place == (k ^ distance), blocks[distance], value)
        rows.append(value)
    return jnp.concatenate(rows, axis=0)


def neighbours(low_out, high_out):
    count = lax.axis_size(LEAF)
    even = lax.axis_index("c") == 0
    pairs = [(i, i + 1) for i in range(1, count - 1, 2)]
    near = sent(jnp.where(even, high_out, low_out), "c", [(0, 1), (1, 0)])
    far = sent(jnp.where(even, low_out, high_out), LEAF, pairs + [(b, a) for a, b in pairs])
    near, far = lax.optimization_barrier((near, far))
    return jnp.where(even, far, near), jnp.where(even, near, far)


def local(
    leaf_value,
    section_cost,
    input_cost,
    dynamics,
    input_map,
    parent_of,
    prob_weight,
    parent_state,
    disturbance,
):
    leaf_dev, slab, states = leaf_value.shape
    par_dev = parent_state.shape[0]
    inputs = input_map.shape[1]
    leaf_index = lax.axis_index(LEAF)
    column = lax.axis_index(MAT)
    core = lax.axis_index("c")
    slot = lax.axis_index("x").astype(jnp.int32)[None]
    row_start = column * slab

    piece = lax.dynamic_slice_in_dim(dynamics, (core * 4 + lax.axis_index("y")) * 128, 128, 1)
    state_rows = jnp.pad(parent_state, ((0, 8 - par_dev), (0, 128 - slab)))
    from_mat = gathered(jnp.concatenate([piece, state_rows], axis=0), MAT)
    state = jnp.moveaxis(from_mat[:, slab : slab + par_dev, :slab], 0, 1).reshape(par_dev, states)

    weights = prob_weight.astype(jnp.float32)
    my_parents = lax.dynamic_slice_in_dim(parent_of, leaf_index * leaf_dev, leaf_dev, 0)
    my_weights = lax.dynamic_slice_in_dim(weights, leaf_index * leaf_dev, leaf_dev, 0)
    first_label = leaf_index * par_dev
    slot_ids = jnp.arange(par_dev + 2, dtype=jnp.int32)
    chosen = (my_parents - first_label + 1)[:, None] == slot_ids[None, :]
    member = jnp.where(chosen, my_weights[:, None], 0.0)
    labels = first_label + jnp.arange(par_dev, dtype=jnp.int32)
    totals = jnp.sum(
        jnp.where(parent_of[:, None] == labels[None, :], weights[:, None], 0.0), axis=0
    )
    terms = jnp.einsum("st,sij->tij", member, leaf_value, precision=HI)
    mapped = jnp.dot(terms.reshape(-1, states), input_map, precision=HI).reshape(par_dev + 2, slab, inputs)
    map_low, map_high = neighbours(mapped[0], mapped[par_dev + 1])
    from_low, from_high = neighbours(terms[0], terms[par_dev + 1])
    input_side = jnp.concatenate([(mapped[1] + map_low) / totals[0], (mapped[2] + map_high) / totals[1]], axis=1)

    line = in_order(exchanged(input_side, "zl"), lax.axis_index("zl"))
    lines = exchanged(line, "x")

    own_dyn = gathered(from_mat, "y")
    other_dyn = sent(own_dyn, "c", [(0, 1), (1, 0)])
    expected = jnp.concatenate([(terms[1] + from_low) / totals[0], (terms[2] + from_high) / totals[1]], axis=0)
    turned, high, low, drift = transition_products(
        core.astype(jnp.int32)[None], own_dyn, other_dyn, expected, jnp.pad(state, ((0, 8 - par_dev), (0, 0)))
    )
    arrived = lax.all_to_all(turned.reshape(states // slab, slab, par_dev * slab), MAT, 0, 0, tiled=True)
    inverse, control = factor_and_control(slot, input_map.T, input_cost, drift, lines, par_dev)

    input_rows = lax.dynamic_slice_in_dim(input_map, row_start, slab, 0)
    following = jnp.einsum("ij,pj->pi", dynamics, state, precision=HI) + jnp.einsum(
        "ia,pa->pi", input_rows, control[:, 0], precision=HI
    )
    even = core == 0
    near = sent(jnp.where(even, following[par_dev - 1 :], following[:1]), "c", [(0, 1), (1, 0)])
    pairs = [(i, i + 1) for i in range(1, lax.axis_size(LEAF) - 1, 2)]
    far = sent(jnp.where(even, following[:1], following[par_dev - 1 :]), LEAF, pairs + [(b, a) for a, b in pairs])
    new_value, gain_rows = value_and_gain(slot, arrived, input_map, inverse, lines, high, low, section_cost)
    near, far, new_value = lax.optimization_barrier((near, far, new_value))
    extended = jnp.concatenate([jnp.where(even, far, near), following, jnp.where(even, near, far)], axis=0)
    child_state = jnp.einsum("st,tj->sj", chosen.astype(jnp.float32), extended, precision=HI) + disturbance
    return (new_value, gain_rows, child_state)


def solution(mesh):
    fine = Mesh(mesh.devices.reshape(4, 4, 2, 4, 4), (*LEAF, *MAT))
    in_specs = (
        P(LEAF, MAT, None),
        P(MAT, None),
        P(),
        P(MAT, None),
        P(),
        P(),
        P(),
        P(LEAF, MAT),
        P(LEAF, MAT),
    )
    out_specs = (P(LEAF, MAT, None), P(LEAF, MAT, None), P(LEAF, MAT))
    return jax.shard_map(local, mesh=fine, in_specs=in_specs, out_specs=out_specs, check_vma=False)
```

```python
import jax
import jax.numpy as jnp
from jax import lax
from jax.experimental import pallas as pl
from jax.experimental.pallas import tpu as pltpu
from jax.sharding import Mesh, PartitionSpec as P

HI = lax.Precision.HIGHEST
LEAF = ("zh", "y", "c")
MAT = ("x", "zl")
BLK = 64


def _panel_step(q, parents, d_ref, cb_ref):
    lane8 = lax.broadcasted_iota(jnp.int32, (8, 128), 0)
    base = pl.multiple_of(q * 8, 8)
    for p in range(parents):
        for c in range(8):
            cb_ref[p, c] = jnp.broadcast_to(d_ref[p, :, c:c + 1], (BLK, 128))
    rows_of = []
    for p in range(parents):
        def element(r, c):
            return jnp.broadcast_to(cb_ref[p, c, pl.ds(base + r, 1), :], (8, 128))

        low = {}
        inv = []
        rows = []
        for c in range(8):
            pivot = element(c, c)
            for t in range(c):
                pivot = pivot - low[c, t] * low[c, t]
            root = lax.rsqrt(pivot)
            root = root * (1.5 - 0.5 * pivot * root * root)
            inv.append(root)
            for r in range(c + 1, 8):
                value = element(r, c)
                for t in range(c):
                    value = value - low[r, t] * low[c, t]
                low[r, c] = value * root
            line = jnp.broadcast_to(d_ref[p, pl.ds(base + c, 1), :], (8, 128))
            for t in range(c):
                line = line - low[c, t] * rows[t]
            rows.append(line * root)
        back = [None] * 8
        for c in range(7, -1, -1):
            line = rows[c]
            for r in range(7, c, -1):
                line = line - low[r, c] * back[r]
            back[c] = line * inv[c]
        block = rows[0]
        for c in range(1, 8):
            block = jnp.where(lane8 == c, rows[c], block)
        rows_of.append((block, back))
    for p in range(parents):
        block, back = rows_of[p]
        for v in range(BLK // 8):
            old = d_ref[p, v * 8:v * 8 + 8, :]
            new = old
            for c in range(8):
                new = new - cb_ref[p, c, v * 8:v * 8 + 8, :] * back[c]
            new = jnp.where(v > q, new, jnp.where(v == q, block, old))
            d_ref[p, v * 8:v * 8 + 8, :] = pltpu.roll(new, 120, 1)


def factor_kernel(h_ref, out_ref, m_ref, d_ref, cb_ref):
    parents, n, _ = h_ref.shape
    row = lax.broadcasted_iota(jnp.int32, (BLK, 128), 0)
    lane = lax.broadcasted_iota(jnp.int32, (BLK, 128), 1)
    unit = jnp.where(lane == row + BLK, 1.0, 0.0)
    full_r = lax.broadcasted_iota(jnp.int32, (n, n), 0)
    full_c = lax.broadcasted_iota(jnp.int32, (n, n), 1)
    for p in range(parents):
        m_ref[p, :, :n] = h_ref[p]
        m_ref[p, :, n:] = jnp.where(full_r == full_c, 1.0, 0.0)
    for k in range(n // BLK):
        top = k * BLK
        lead = (top // 128) * 128
        stop = n + ((top + BLK + 127) // 128) * 128
        for p in range(parents):
            tile = m_ref[p, top:top + BLK, lead:lead + 128]
            if top != lead:
                tile = pltpu.roll(tile, 128 - (top - lead), 1)
            d_ref[p] = jnp.where(lane < BLK, tile, unit)
        lax.fori_loop(0, BLK // 8, lambda q, _: (_panel_step(q, parents, d_ref, cb_ref), 0)[1], 0)
        for p in range(parents):
            inverse = d_ref[p][:, :BLK]
            scaled = jnp.dot(inverse, m_ref[p, top:top + BLK, lead:stop], precision=HI, preferred_element_type=jnp.float32)
            m_ref[p, top:top + BLK, lead:stop] = scaled
            if top + BLK < n:
                left = jnp.transpose(scaled[:, :n - lead])
                left = left[top + BLK - lead:, :]
                m_ref[p, top + BLK:, lead:stop] = m_ref[p, top + BLK:, lead:stop] - jnp.dot(
                    left, scaled, precision=HI, preferred_element_type=jnp.float32)
    for p in range(parents):
        out_ref[p] = m_ref[p, :, n:]


def split(value):
    high = value.astype(jnp.bfloat16)
    return high, (value - high.astype(jnp.float32)).astype(jnp.bfloat16)


def three_pass(left, right, dims=(((1,), (0,)), ((), ()))):
    def part(a, b):
        return lax.dot_general(a, b, dims, preferred_element_type=jnp.float32)

    return part(left[0], right[1]) + part(left[1], right[0]) + part(left[0], right[0])


def exact(left, right, dims=(((1,), (0,)), ((), ()))):
    return lax.dot_general(left, right, dims, precision=HI, preferred_element_type=jnp.float32)


CROSS = (((1,), (1,)), ((), ()))


def piece_of(step, core):
    return jnp.where(step < 4, core * 4 + step, (1 - core) * 4 + step - 4)


def transition_kernel(core_ref, own_ref, other_ref, value_ref, state_ref, turned_ref, high_ref, low_ref, drift_ref, vh_ref, vl_ref):
    step = pl.program_id(0)
    states = value_ref.shape[1]

    @pl.when(step == 0)
    def _():
        vh_ref[...], vl_ref[...] = split(value_ref[...])
        drift_ref[...] = jnp.zeros_like(drift_ref)

    piece = jnp.where(step < 4, own_ref[0, :, :64, :], other_ref[0, :, :64, :]).reshape(states, 128)
    high, low = split(piece)
    high_ref[...] = high
    low_ref[...] = low
    turned_ref[...] = jnp.transpose(three_pass((vh_ref[...], vl_ref[...]), (high, low)))
    drift_ref[...] += three_pass(split(state_ref[...]), (high, low), CROSS)


def transition_products(core, own, other, value, state):
    states = value.shape[1]
    rows = own.shape[1:]
    grid = pltpu.PrefetchScalarGridSpec(
        num_scalar_prefetch=1,
        grid=(8,),
        in_specs=[
            pl.BlockSpec((1, *rows), lambda s, c: (jnp.minimum(s, 3), 0, 0, 0)),
            pl.BlockSpec((1, *rows), lambda s, c: (jnp.maximum(s - 4, 0), 0, 0, 0)),
            pl.BlockSpec(value.shape, lambda s, c: (0, 0)),
            pl.BlockSpec((8, 128), lambda s, c: (0, piece_of(s, c[0]))),
        ],
        out_specs=[
            pl.BlockSpec((128, 128), lambda s, c: (piece_of(s, c[0]), 0)),
            pl.BlockSpec((states, 128), lambda s, c: (0, piece_of(s, c[0]))),
            pl.BlockSpec((states, 128), lambda s, c: (0, piece_of(s, c[0]))),
            pl.BlockSpec((8, states), lambda s, c: (0, 0)),
        ],
        scratch_shapes=[
            pltpu.VMEM(value.shape, jnp.bfloat16),
            pltpu.VMEM(value.shape, jnp.bfloat16),
        ],
    )
    return pl.pallas_call(
        transition_kernel,
        grid_spec=grid,
        out_shape=[
            jax.ShapeDtypeStruct((states, 128), jnp.float32),
            jax.ShapeDtypeStruct((states, states), jnp.bfloat16),
            jax.ShapeDtypeStruct((states, states), jnp.bfloat16),
            jax.ShapeDtypeStruct((8, states), jnp.float32),
        ],
        cost_estimate=pl.CostEstimate(flops=10**9, bytes_accessed=14 * 10**6, transcendentals=0),
    )(core, own, other, value, state)


def blocks_of(slot_ref, line_refs):
    return [(pl.multiple_of((slot_ref[0] ^ k) * 256, 256), ref) for k, ref in enumerate(line_refs)]


def hessian_kernel(slot_ref, turned_map_ref, cost_ref, drift_ref, line0, line1, line2, line3, out_ref, control_ref, h_ref, m_ref, d_ref, cb_ref):
    n = cost_ref.shape[0]
    parents = out_ref.shape[0]
    total = None
    pull = None
    for start, ref in blocks_of(slot_ref, (line0, line1, line2, line3)):
        rows = ref.shape[0]
        term = exact(turned_map_ref[:, pl.ds(start, rows)], ref[...])
        total = term if total is None else total + term
        share = exact(drift_ref[:, pl.ds(start, rows)], ref[...])
        pull = share if pull is None else pull + share
    for p in range(parents):
        h_ref[p] = cost_ref[...] + total[:, p * n : (p + 1) * n]
    factor_kernel(h_ref, out_ref, m_ref, d_ref, cb_ref)
    for p in range(parents):
        coupled = pull[:, p * n : (p + 1) * n]
        control_ref[p] = -exact(exact(coupled, out_ref[p], CROSS), out_ref[p])


def factor_and_control(slot, turned_map, cost, drift, lines, parents):
    n = cost.shape[0]
    vmem = pl.BlockSpec(memory_space=pltpu.VMEM)
    return pl.pallas_call(
        hessian_kernel,
        in_specs=[pl.BlockSpec(memory_space=pltpu.SMEM)] + [vmem] * 7,
        out_specs=[vmem] * 2,
        out_shape=[
            jax.ShapeDtypeStruct((parents, n, n), jnp.float32),
            jax.ShapeDtypeStruct((parents, 8, n), jnp.float32),
        ],
        scratch_shapes=[
            pltpu.VMEM((parents, n, n), jnp.float32),
            pltpu.VMEM((parents, n, 2 * n), jnp.float32),
            pltpu.VMEM((parents, BLK, 128), jnp.float32),
            pltpu.VMEM((parents, 8, BLK, 128), jnp.float32),
        ],
        cost_estimate=pl.CostEstimate(flops=10**10, bytes_accessed=4 * 10**6, transcendentals=0),
    )(slot, turned_map, cost, drift, *lines)


def value_kernel(slot_ref, arrived_ref, map_ref, inverse_ref, line0, line1, line2, line3, high_hbm, low_hbm, section_ref, value_ref, gain_ref, cols_ref, high_ref, low_ref, sem_ref):
    copies = [pltpu.make_async_copy(high_hbm, high_ref, sem_ref.at[0]), pltpu.make_async_copy(low_hbm, low_ref, sem_ref.at[1])]
    for copy in copies:
        copy.start()
    parents, slab, n = gain_ref.shape
    states = section_ref.shape[1]
    lane = lax.broadcasted_iota(jnp.int32, (slab, 128), 1)
    for i in range(states // 128):
        even, odd = arrived_ref[2 * i], arrived_ref[2 * i + 1]
        cols_ref[:slab, i * 128 : (i + 1) * 128] = jnp.where(lane < 64, even, pltpu.roll(odd, 64, 1))
        cols_ref[slab:, i * 128 : (i + 1) * 128] = jnp.where(lane < 64, pltpu.roll(even, 64, 1), odd)
    coupling = three_pass(split(cols_ref[...]), split(map_ref[...]))
    for p in range(parents):
        rows = slice(p * slab, (p + 1) * slab)
        gain = -exact(exact(coupling[rows], inverse_ref[p], CROSS), inverse_ref[p])
        gain_ref[p] = gain
        for start, ref in blocks_of(slot_ref, (line0, line1, line2, line3)):
            count = ref.shape[0]
            change = three_pass(split(gain), split(ref[:, p * n : (p + 1) * n]), CROSS)
            cols_ref[rows, pl.ds(start, count)] = cols_ref[rows, pl.ds(start, count)] + change
    left = split(cols_ref[...])
    for copy in copies:
        copy.wait()
    for j in range(states // 256):
        span = slice(j * 256, (j + 1) * 256)
        part = three_pass(left, (high_ref[:, span], low_ref[:, span]))
        for p in range(parents):
            value_ref[p, :, span] = section_ref[:, span] + part[p * slab : (p + 1) * slab]


def value_and_gain(slot, arrived, input_map, inverse, lines, high, low, section):
    parents, n, _ = inverse.shape
    slab, states = section.shape
    vmem = pl.BlockSpec(memory_space=pltpu.VMEM)
    return pl.pallas_call(
        value_kernel,
        in_specs=[pl.BlockSpec(memory_space=pltpu.SMEM)] + [vmem] * 7 + [pl.BlockSpec(memory_space=pl.ANY)] * 2 + [vmem],
        out_specs=[vmem] * 2,
        out_shape=[
            jax.ShapeDtypeStruct((parents, slab, states), jnp.float32),
            jax.ShapeDtypeStruct((parents, slab, n), jnp.float32),
        ],
        scratch_shapes=[
            pltpu.VMEM((parents * slab, states), jnp.float32),
            pltpu.VMEM((states, states), jnp.bfloat16),
            pltpu.VMEM((states, states), jnp.bfloat16),
            pltpu.SemaphoreType.DMA((2,)),
        ],
        cost_estimate=pl.CostEstimate(flops=3 * 10**9, bytes_accessed=8 * 10**6, transcendentals=0),
    )(slot, arrived, input_map, inverse, *lines, high, low, section)


def gathered(shard, axis):
    peers = lax.axis_size(axis)
    return lax.all_to_all(jnp.broadcast_to(shard[None], (peers, *shard.shape)), axis, 0, 0, tiled=True)


def sent(value, axis, pairs):
    return lax.ppermute(value, axis, pairs)


def exchanged(shard, axis):
    return [shard] + [sent(shard, axis, [(i, i ^ k) for i in range(4)]) for k in (1, 2, 3)]


def in_order(blocks, place):
    rows = []
    for k in range(4):
        value = blocks[3]
        for distance in (2, 1, 0):
            value = jnp.where(place == (k ^ distance), blocks[distance], value)
        rows.append(value)
    return jnp.concatenate(rows, axis=0)


def neighbours(low_out, high_out):
    count = lax.axis_size(LEAF)
    even = lax.axis_index("c") == 0
    pairs = [(i, i + 1) for i in range(1, count - 1, 2)]
    near = sent(jnp.where(even, high_out, low_out), "c", [(0, 1), (1, 0)])
    far = sent(jnp.where(even, low_out, high_out), LEAF, pairs + [(b, a) for a, b in pairs])
    near, far = lax.optimization_barrier((near, far))
    return jnp.where(even, far, near), jnp.where(even, near, far)


def local(
    leaf_value,
    section_cost,
    input_cost,
    dynamics,
    input_map,
    parent_of,
    prob_weight,
    parent_state,
    disturbance,
):
    leaf_dev, slab, states = leaf_value.shape
    par_dev = parent_state.shape[0]
    inputs = input_map.shape[1]
    leaf_index = lax.axis_index(LEAF)
    column = lax.axis_index(MAT)
    core = lax.axis_index("c")
    slot = lax.axis_index("x").astype(jnp.int32)[None]
    row_start = column * slab

    piece = lax.dynamic_slice_in_dim(dynamics, (core * 4 + lax.axis_index("y")) * 128, 128, 1)
    state_rows = jnp.pad(parent_state, ((0, 8 - par_dev), (0, 128 - slab)))
    from_mat = gathered(jnp.concatenate([piece, state_rows], axis=0), MAT)
    state = jnp.moveaxis(from_mat[:, slab : slab + par_dev, :slab], 0, 1).reshape(par_dev, states)

    weights = prob_weight.astype(jnp.float32)
    my_parents = lax.dynamic_slice_in_dim(parent_of, leaf_index * leaf_dev, leaf_dev, 0)
    my_weights = lax.dynamic_slice_in_dim(weights, leaf_index * leaf_dev, leaf_dev, 0)
    first_label = leaf_index * par_dev
    slot_ids = jnp.arange(par_dev + 2, dtype=jnp.int32)
    chosen = (my_parents - first_label + 1)[:, None] == slot_ids[None, :]
    member = jnp.where(chosen, my_weights[:, None], 0.0)
    labels = first_label + jnp.arange(par_dev, dtype=jnp.int32)
    totals = jnp.sum(
        jnp.where(parent_of[:, None] == labels[None, :], weights[:, None], 0.0), axis=0
    )
    terms = jnp.einsum("st,sij->tij", member, leaf_value, precision=HI)
    mapped = jnp.dot(terms.reshape(-1, states), input_map, precision=HI).reshape(par_dev + 2, slab, inputs)
    map_low, map_high = neighbours(mapped[0], mapped[par_dev + 1])
    from_low, from_high = neighbours(terms[0], terms[par_dev + 1])
    input_side = jnp.concatenate([(mapped[1] + map_low) / totals[0], (mapped[2] + map_high) / totals[1]], axis=1)

    line = in_order(exchanged(input_side, "zl"), lax.axis_index("zl"))
    lines = exchanged(line, "x")

    own_dyn = gathered(from_mat, "y")
    expected = jnp.concatenate([(terms[1] + from_low) / totals[0], (terms[2] + from_high) / totals[1]], axis=0)
    padded = jnp.pad(state, ((0, 8 - par_dev), (0, 0)))
    own_drift = jnp.einsum("ij,pj->pi", dynamics, state, precision=HI)
    own_dyn, expected, padded, own_drift, turned_map = lax.optimization_barrier(
        (own_dyn, expected, padded, own_drift, input_map.T)
    )
    other_dyn = sent(own_dyn, "c", [(0, 1), (1, 0)])
    turned, high, low, drift = transition_products(
        core.astype(jnp.int32)[None], own_dyn, other_dyn, expected, padded
    )
    arrived = lax.all_to_all(turned.reshape(states // slab, slab, par_dev * slab), MAT, 0, 0, tiled=True)
    inverse, control = factor_and_control(slot, turned_map, input_cost, drift, lines, par_dev)

    input_rows = lax.dynamic_slice_in_dim(input_map, row_start, slab, 0)
    following = own_drift + jnp.einsum(
        "ia,pa->pi", input_rows, jnp.stack([control[p, p] for p in range(par_dev)]), precision=HI
    )
    even = core == 0
    near = sent(jnp.where(even, following[par_dev - 1 :], following[:1]), "c", [(0, 1), (1, 0)])
    pairs = [(i, i + 1) for i in range(1, lax.axis_size(LEAF) - 1, 2)]
    far = sent(jnp.where(even, following[:1], following[par_dev - 1 :]), LEAF, pairs + [(b, a) for a, b in pairs])
    new_value, gain_rows = value_and_gain(slot, arrived, input_map, inverse, lines, high, low, section_cost)
    near, far, new_value = lax.optimization_barrier((near, far, new_value))
    extended = jnp.concatenate([jnp.where(even, far, near), following, jnp.where(even, near, far)], axis=0)
    child_state = jnp.einsum("st,tj->sj", chosen.astype(jnp.float32), extended, precision=HI) + disturbance
    return (new_value, gain_rows, child_state)


def solution(mesh):
    fine = Mesh(mesh.devices.reshape(4, 4, 2, 4, 4), (*LEAF, *MAT))
    in_specs = (
        P(LEAF, MAT, None),
        P(MAT, None),
        P(),
        P(MAT, None),
        P(),
        P(),
        P(),
        P(LEAF, MAT),
        P(LEAF, MAT),
    )
    out_specs = (P(LEAF, MAT, None), P(LEAF, MAT, None), P(LEAF, MAT))
    return jax.shard_map(local, mesh=fine, in_specs=in_specs, out_specs=out_specs, check_vma=False)
```
